32 devices in a mesh: gx: 8 (over z, core), gy: 4 (over y, x).
Axes of the slice: x: 2, y: 2, z: 4, core: 2. Of those that a mesh axis runs over, the one named last changes fastest.
Arguments:
- proof: bfloat16 [2048, 256, 512], P(('gx', 'gy')), may hold values from -6 to 6
- target: bfloat16 [64, 256, 512], P('gx', 'gy'), may hold values from -6 to 6
- loading: float32 [256], replicated, may hold values from 2 to 32
Outputs:
- predicted: float32 [64, 256, 512], P('gx', 'gy')
The draws below stay inside these ranges and needn't reach their ends.
All inputs are finite; a program needn't handle non-finite values.
Results may differ from the reference program's by a relative error of at most 0.0049.
The reference program's roundings to bfloat16 on the way count: a program that leaves them out, or rounds other values in their place, can miss the bound.
Values may be sent and summed in bfloat16 or wider, within the bound.
No kernel may reach another device: no remote copies, remote signals or barrier semaphores. Data moves between devices by JAX's collectives and lax.ppermute only.
A program may use at most 192 MiB of HBM per device.

```python
import math
import jax
import jax.numpy as jnp
from jax import lax

W = 2048
P_SIZE = 64
L = 512
S = 256
F = 256


def strengthened(drawn, stream_key, source, target, blocks, factor):
    owner, partner = [(jnp.arange(drawn.shape[dim]) // (drawn.shape[dim] // blocks)).reshape([-1 if axis == dim else 1 for axis in range(drawn.ndim)]) for dim in (source, target)]
    chosen = jax.random.permutation(stream_key, blocks)[partner]
    strong = (owner == chosen) | (owner == (partner + blocks // 2) % blocks)
    return jnp.where(strong, factor * drawn, drawn)


def levels(rng, extent, shards, least, largest):
    def one(position, blocks):
        draws = jax.random.uniform(jax.random.fold_in(jax.random.fold_in(rng, 6), position), (blocks,), jnp.float32, least / len(shards), largest / len(shards))
        return jnp.repeat(jnp.exp(draws), extent[position] // blocks).reshape((-1,) + (1,) * (len(extent) - position - 1))

    loudness = one(*shards[0])
    for cut in shards[1:]:
        loudness = loudness * one(*cut)
    return loudness


def bell_draw(key, dims, deviation, bound, cuts=(), kind=jnp.bfloat16):
    drawn = jax.random.normal(key, dims, jnp.float32) * deviation
    if len(cuts) > 0:
        drawn = levels(key, dims, cuts, -0.22, 0.18) * drawn
    return jnp.clip(drawn, min=-bound, max=bound).astype(kind)


def noise_with(key, extent, deviation, bound, split, heavy, kind=jnp.bfloat16):
    entries = deviation * jax.random.normal(key, extent, jnp.float32)
    if split:
        entries = entries * levels(key, extent, split, -0.22, 0.18)
    return jnp.clip(strengthened(entries, jax.random.fold_in(key, 3), *heavy), -bound, bound).astype(kind)


def setup_inputs(seed: int = 0) -> dict:
    key_of = jax.random.split(jax.random.key(seed), 4)
    return {
        "proof": noise_with(key_of[0], (W, S, L), 1.0, 6.0, ((0, 32),), (0, 1, 32, 2.75)),
        "target": bell_draw(key_of[1], (P_SIZE, S, L), 1.0, 6.0, ((0, 8), (1, 4))),
        "loading": jnp.clip(jnp.exp(jax.random.uniform(key_of[2], (F,), jnp.float32, math.log(2.0), math.log(32.0))), 2.0, 32.0),
    }


def transform_tables(length):
    half = length // 2
    sample = jnp.arange(length, dtype=jnp.int32)
    freq_bin = jnp.arange(half, dtype=jnp.int32)
    phase = (freq_bin[:, None] * sample[None, :] % length).astype(jnp.float32) * (2.0 * math.pi / length)
    window = 0.5 - 0.5 * jnp.cos(sample.astype(jnp.float32) * (2.0 * math.pi / length))
    forward = jnp.stack([window * jnp.cos(phase), -window * jnp.sin(phase)], axis=1).reshape(length, length)
    forward = forward * (1.0 / math.sqrt(0.375 * length))
    inverse = jnp.stack([jnp.cos(phase), -jnp.sin(phase)], axis=1).reshape(length, length) * math.sqrt(2.0 / length)
    return (forward.astype(jnp.bfloat16), inverse.astype(jnp.bfloat16))

def contract(left, right):
    return lax.dot_general(left, right, (((1,), (1,)), ((), ())), preferred_element_type=jnp.float32)

def project(left, right):
    return lax.dot_general(left, right, (((0,), (0,)), ((), ())), preferred_element_type=jnp.float32)

def reference(proof, target, loading):
    length = proof.shape[2]
    channels = proof.shape[0]
    targets = target.shape[0]
    segments = proof.shape[1]
    forward, inverse = transform_tables(length)
    wit_spec = lax.dot_general(forward, proof, (((1,), (2,)), ((), ())), preferred_element_type=jnp.float32).astype(jnp.bfloat16)
    tar_spec = lax.dot_general(forward, target, (((1,), (2,)), ((), ())), preferred_element_type=jnp.float32).astype(jnp.bfloat16)
    wit_bins = wit_spec.reshape(length // 2, 2, channels, segments)
    tar_bins = tar_spec.reshape(length // 2, 2, targets, segments)
    rho = (1.0 + math.sqrt(channels / segments)) ** 2

    def per_bin(items):
        wit, tar, load_val = items
        wit_re, wit_im = (wit[0], wit[1])
        tar_re, tar_im = (tar[0], tar[1])
        gram_re = ((contract(wit_re, wit_re) + contract(wit_im, wit_im)) / segments).astype(jnp.bfloat16)
        gram_im = ((contract(wit_im, wit_re) - contract(wit_re, wit_im)) / segments).astype(jnp.bfloat16)
        rhs_re = (contract(wit_re, tar_re) + contract(wit_im, tar_im)) / segments
        rhs_im = (contract(wit_im, tar_re) - contract(wit_re, tar_im)) / segments
        step_size = 1.0 / (load_val + rho)
        first_re = step_size * rhs_re
        first_im = step_size * rhs_im
        half_re = first_re.astype(jnp.bfloat16)
        half_im = first_im.astype(jnp.bfloat16)
        image_re = jnp.dot(gram_re, half_re, preferred_element_type=jnp.float32) - jnp.dot(gram_im, half_im, preferred_element_type=jnp.float32)
        image_im = jnp.dot(gram_re, half_im, preferred_element_type=jnp.float32) + jnp.dot(gram_im, half_re, preferred_element_type=jnp.float32)
        second_re = (first_re + step_size * (rhs_re - image_re - load_val * first_re)).astype(jnp.bfloat16)
        second_im = (first_im + step_size * (rhs_im - image_im - load_val * first_im)).astype(jnp.bfloat16)
        pred_re = project(second_re, wit_re) + project(second_im, wit_im)
        pred_im = project(second_re, wit_im) - project(second_im, wit_re)
        return jnp.stack([pred_re, pred_im]).astype(jnp.bfloat16)
    preds = lax.map(per_bin, (wit_bins, tar_bins, loading))
    preds = preds.reshape(length, targets, segments)
    return lax.dot_general(preds, inverse, (((0,), (0,)), ((), ())), preferred_element_type=jnp.float32)
```

```python
import functools
import math

import jax
import jax.numpy as jnp
import numpy as np
from jax import lax
from jax.experimental import pallas as pl
from jax.experimental.pallas import tpu as pltpu
from jax.sharding import PartitionSpec as P

AXES = ("gx", "gy")
LANES = 128
VMEM = 60 * 1024 * 1024


def forward_rows(bins, length):
    sample = jnp.arange(length, dtype=jnp.int32)
    phase = (bins[:, None] * sample[None, :] % length).astype(jnp.float32) * (
        2.0 * math.pi / length
    )
    window = 0.5 - 0.5 * jnp.cos(sample.astype(jnp.float32) * (2.0 * math.pi / length))
    rows = jnp.stack([window * jnp.cos(phase), -window * jnp.sin(phase)], axis=1)
    rows = rows.reshape(2 * bins.shape[0], length) * (1.0 / math.sqrt(0.375 * length))
    return rows.astype(jnp.bfloat16)


def inverse_table(length):
    half = length // 2
    sample = jnp.arange(length, dtype=jnp.int32)
    freq_bin = jnp.arange(half, dtype=jnp.int32)
    phase = (freq_bin[:, None] * sample[None, :] % length).astype(jnp.float32) * (
        2.0 * math.pi / length
    )
    table = jnp.stack([jnp.cos(phase), -jnp.sin(phase)], axis=1).reshape(length, length)
    return (table * math.sqrt(2.0 / length)).astype(jnp.bfloat16)


def nt(left, right):
    return lax.dot_general(
        left, right, (((1,), (1,)), ((), ())), preferred_element_type=jnp.float32
    )


def nn(left, right):
    return lax.dot_general(
        left, right, (((1,), (0,)), ((), ())), preferred_element_type=jnp.float32
    )


def tn(left, right):
    return lax.dot_general(
        left, right, (((0,), (0,)), ((), ())), preferred_element_type=jnp.float32
    )


def spectra_kernel(block, rows, sizes, table_ref, wave_ref, *refs):
    outs, scratch = refs[:-1], refs[-1]
    strips = scratch.shape[0]
    for channel in range(block):
        spec = nt(table_ref[...], wave_ref[channel])
        for strip in range(strips):
            scratch[strip, pl.ds(channel, rows, stride=block), :] = spec[
                :, strip * LANES : (strip + 1) * LANES
            ]
    start = 0
    for out, size in zip(outs, sizes):
        for strip in range(strips):
            span = scratch[strip, pl.ds(start * block, size * block), :]
            out[:, :, strip * LANES : (strip + 1) * LANES] = span.reshape(
                size, block, LANES
            ).astype(out.dtype)
        start += size


def spectra(table, wave, sizes):
    rows, length = table.shape
    channels, segments, _ = wave.shape
    block = min(16, channels)
    return pl.pallas_call(
        functools.partial(spectra_kernel, block, rows, sizes),
        grid=(channels // block,),
        in_specs=[
            pl.BlockSpec((rows, length), lambda i: (0, 0)),
            pl.BlockSpec((block, segments, length), lambda i: (i, 0, 0)),
        ],
        out_specs=[pl.BlockSpec((size, block, segments), lambda i: (0, i, 0)) for size in sizes],
        out_shape=[
            jax.ShapeDtypeStruct((size, channels, segments), jnp.bfloat16) for size in sizes
        ],
        scratch_shapes=[pltpu.VMEM((segments // LANES, rows * block, LANES), jnp.float32)],
        compiler_params=pltpu.CompilerParams(vmem_limit_bytes=VMEM),
        cost_estimate=pl.CostEstimate(
            flops=2 * rows * length * channels * segments,
            bytes_accessed=2 * channels * segments * (length + rows),
            transcendentals=0,
        ),
        name="spectra",
    )(table, wave)


def packed_gram(pieces, scale):
    real = jnp.concatenate([piece[0] for piece in pieces], axis=0)
    imag = jnp.concatenate([piece[1] for piece in pieces], axis=0)
    left = jnp.concatenate([real, imag], axis=0)
    turned = jnp.concatenate([imag, -real], axis=0)
    return (tn(left, left) + tn(left, turned)) * scale


def gram_kernel(pieces, scale, heads, *refs):
    ins, extra, outs = refs[:pieces], refs[pieces:-heads], refs[-heads:]
    size = ins[0].shape[0] // 2
    for place in range(size):
        total = packed_gram([ref[2 * place : 2 * place + 2] for ref in ins], scale)
        for ref in extra:
            total = total + ref[place].astype(jnp.float32)
        if heads == 2 and place >= size // 2:
            outs[1][place - size // 2] = total.astype(outs[1].dtype)
        else:
            outs[0][place] = total.astype(outs[0].dtype)


def gram(pieces, start, count, scale, extra, out_types):
    _, channels, segments = pieces[0].shape
    heads = len(out_types)
    each = count // heads
    spec = pl.BlockSpec((2 * count, channels, segments), lambda i: (start // count, 0, 0))
    whole = pl.BlockSpec((count, segments, segments), lambda i: (0, 0, 0))
    return pl.pallas_call(
        functools.partial(gram_kernel, len(pieces), scale, heads),
        grid=(1,),
        in_specs=[spec] * len(pieces) + [whole] * len(extra),
        out_specs=[pl.BlockSpec((each, segments, segments), lambda i: (0, 0, 0))] * heads,
        out_shape=[jax.ShapeDtypeStruct((each, segments, segments), kind) for kind in out_types],
        compiler_params=pltpu.CompilerParams(vmem_limit_bytes=VMEM),
        cost_estimate=pl.CostEstimate(
            flops=8 * count * len(pieces) * channels * segments * segments,
            bytes_accessed=4 * count * len(pieces) * channels * segments
            + 4 * count * segments * segments,
            transcendentals=0,
        ),
        name="gram",
    )(*pieces, *extra)


def split(value):
    high = value.astype(jnp.bfloat16)
    return high, (value - high.astype(jnp.float32)).astype(jnp.bfloat16)


def times_gram(real, imag, high, low):
    rows = real.shape[0]
    vec_high, vec_low = split(jnp.concatenate([real, imag], axis=0))
    straight = nn(vec_high, high) + nn(vec_low, high) + nn(vec_high, low)
    turned = nt(vec_high, high) + nt(vec_low, high) + nt(vec_high, low)
    first, second = straight[:rows], straight[rows:]
    third, fourth = turned[:rows], turned[rows:]
    out_re = 0.5 * (first - second + third + fourth)
    out_im = 0.5 * (first + second + fourth - third)
    return out_re, out_im


def predict_kernel(count, loads_ref, mine_ref, *refs):
    extra, tar_ref, out_ref = refs[:-2], refs[-2], refs[-1]
    for place in range(count):
        packed = mine_ref[place].astype(jnp.float32)
        for ref in extra:
            packed = packed + ref[place].astype(jnp.float32)
        high, low = split(packed)
        alpha = loads_ref[0, place]
        beta = loads_ref[1, place]
        tar_re = tar_ref[2 * place].astype(jnp.float32)
        tar_im = tar_ref[2 * place + 1].astype(jnp.float32)
        once_re, once_im = times_gram(tar_re, tar_im, high, low)
        pred_re, pred_im = times_gram(
            alpha * tar_re - beta * once_re, alpha * tar_im - beta * once_im, high, low
        )
        out_ref[2 * place] = pred_re.astype(out_ref.dtype)
        out_ref[2 * place + 1] = pred_im.astype(out_ref.dtype)


def predict(coefs, mine, extra, tar):
    count, segments, _ = mine.shape
    targets = tar.shape[1]
    whole = pl.BlockSpec((count, segments, segments), lambda i: (0, 0, 0))
    pair = pl.BlockSpec((2 * count, targets, segments), lambda i: (0, 0, 0))
    return pl.pallas_call(
        functools.partial(predict_kernel, count),
        grid=(1,),
        in_specs=[pl.BlockSpec(memory_space=pltpu.SMEM), whole] + [whole] * len(extra) + [pair],
        out_specs=pair,
        out_shape=jax.ShapeDtypeStruct((2 * count, targets, segments), jnp.bfloat16),
        compiler_params=pltpu.CompilerParams(vmem_limit_bytes=VMEM),
        name="predict",
    )(coefs, mine, *extra, tar)


def bit_list(number):
    return [1 << place for place in range(number.bit_length() - 1)]


def masks_of(bits):
    out = [0]
    for bit in bits:
        out = [mask | turn for mask in out for turn in (0, bit)]
    return out


def build_plan(outer, inner, channels, segments, per_device):
    low = bit_list(inner)
    high = [bit * inner for bit in bit_list(outer)]
    orders = [high[:1] + low + high[1:], high[:1] + low[::-1] + high[1:]]
    traded, held = 0, channels
    while traded < len(low) + len(high) and 2 * held <= segments:
        traded, held = traded + 1, 2 * held
    plan = []
    for number in range(per_device):
        order = orders[number % len(orders)]
        plan.append((number, 1, order[:traded], order[traded:]))
    return plan


def local(devices, outer, inner, proof, target, loading):
    channels, segments, length = proof.shape
    targets, span = target.shape[0], target.shape[1]
    half = length // 2
    per_device = half // devices
    rho = (1.0 + math.sqrt(channels * devices / segments)) ** 2
    me = lax.axis_index(AXES)
    plan = build_plan(outer, inner, channels, segments, per_device)

    def swap(value, mask):
        pairs = [(place, place ^ mask) for place in range(devices)]
        return lax.ppermute(value, AXES, pairs)

    flips, offsets = [], []
    for first, count, traded, summed in plan:
        for mask in masks_of(traded):
            for rest in masks_of(summed):
                for place in range(count):
                    flips.append(mask | rest)
                    offsets.append(first + place)
    bins = jnp.bitwise_xor(me, jnp.asarray(np.array(flips, np.int32))) * per_device + jnp.asarray(
        np.array(offsets, np.int32)
    )
    table = forward_rows(bins, length)
    natural = forward_rows(jnp.arange(half, dtype=jnp.int32), length)

    sizes = []
    for first, count, traded, summed in plan:
        sizes += [2 * count * 2 ** len(summed)] * 2 ** len(traded)
    pieces = spectra(table, proof, sizes)

    tar_spec = lax.dot_general(
        natural, target, (((1,), (2,)), ((), ())), preferred_element_type=jnp.float32
    ).astype(jnp.bfloat16)
    tar = lax.all_to_all(tar_spec, AXES, split_axis=0, concat_axis=0, tiled=True)
    tar = tar.reshape(outer, inner, 2 * per_device, targets, span)
    tar = tar.transpose(2, 0, 3, 1, 4).reshape(2 * per_device, outer * targets, inner * span)

    mine = lax.dynamic_slice_in_dim(loading, me * per_device, per_device)
    step = 1.0 / (mine + rho)
    coefs = jnp.stack([step * (2.0 - step * mine), step * step])

    held = []
    at = 0
    for first, count, traded, summed in plan:
        masks = masks_of(traded)
        got = [pieces[at]] + [
            swap(pieces[at + number], mask) for number, mask in enumerate(masks) if mask
        ]
        at += len(masks)
        held.append(got)

    preds = []
    scale = 1.0 / segments
    for (first, count, traded, summed), got in zip(plan, held):
        total = count * 2 ** len(summed)
        if not summed:
            (keep,) = gram(got, 0, total, scale, (), (jnp.float32,))
            extra = ()
        else:
            (send,) = gram(got, total // 2, total // 2, scale, (), (jnp.bfloat16,))
            came = swap(send, summed[0])
            if len(summed) == 1:
                (keep,) = gram(got, 0, total // 2, scale, (came,), (jnp.float32,))
                extra = ()
            else:
                keep, send = gram(
                    got, 0, total // 2, scale, (came,), (jnp.float32, jnp.bfloat16)
                )
                for bit in summed[1:-1]:
                    came = swap(send, bit)
                    both = keep + came.astype(jnp.float32)
                    middle = both.shape[0] // 2
                    keep, send = both[:middle], both[middle:].astype(jnp.bfloat16)
                extra = (swap(send, summed[-1]),)
        rows = slice(2 * first, 2 * (first + count))
        preds.append(predict(coefs[:, first : first + count], keep, extra, tar[rows]))

    pred = jnp.concatenate(preds, axis=0)
    pred = pred.reshape(2 * per_device, outer, targets, inner, span).transpose(1, 3, 0, 2, 4)
    pred = pred.reshape(devices * 2 * per_device, targets, span)
    returned = lax.all_to_all(pred, AXES, split_axis=0, concat_axis=0, tiled=True)
    return lax.dot_general(
        returned,
        inverse_table(length),
        (((0,), (0,)), ((), ())),
        preferred_element_type=jnp.float32,
    )


def solution(mesh):
    outer, inner = mesh.shape["gx"], mesh.shape["gy"]
    return jax.shard_map(
        functools.partial(local, outer * inner, outer, inner),
        mesh=mesh,
        in_specs=(P(AXES, None, None), P("gx", "gy", None), P()),
        out_specs=P("gx", "gy", None),
        check_vma=False,
    )
```

```python
import functools
import math

import jax
import jax.numpy as jnp
import numpy as np
from jax import lax
from jax.experimental import pallas as pl
from jax.experimental.pallas import tpu as pltpu
from jax.sharding import PartitionSpec as P

AXES = ("gx", "gy")
LANES = 128
VMEM = 60 * 1024 * 1024


def forward_rows(bins, length):
    sample = np.arange(length, dtype=np.int64)
    phase = ((bins[:, None] * sample[None, :]) % length).astype(np.float32) * np.float32(
        2.0 * math.pi / length
    )
    window = np.float32(0.5) - np.float32(0.5) * np.cos(
        sample.astype(np.float32) * np.float32(2.0 * math.pi / length)
    )
    rows = np.stack([window * np.cos(phase), -window * np.sin(phase)], axis=1)
    rows = rows.reshape(2 * bins.shape[0], length) * np.float32(1.0 / math.sqrt(0.375 * length))
    return jnp.asarray(rows.astype(jnp.bfloat16))


def inverse_table(length):
    sample = np.arange(length, dtype=np.int64)
    bins = np.arange(length // 2, dtype=np.int64)
    phase = ((bins[:, None] * sample[None, :]) % length).astype(np.float32) * np.float32(
        2.0 * math.pi / length
    )
    table = np.stack([np.cos(phase), -np.sin(phase)], axis=1).reshape(length, length)
    return jnp.asarray((table * np.float32(math.sqrt(2.0 / length))).astype(jnp.bfloat16))


def nt(left, right):
    return lax.dot_general(
        left, right, (((1,), (1,)), ((), ())), preferred_element_type=jnp.float32
    )


def nn(left, right):
    return lax.dot_general(
        left, right, (((1,), (0,)), ((), ())), preferred_element_type=jnp.float32
    )


def tn(left, right):
    return lax.dot_general(
        left, right, (((0,), (0,)), ((), ())), preferred_element_type=jnp.float32
    )


def spectra_kernel(block, owners, jobs, order_ref, table_ref, wave_ref, *refs):
    outs, scratch = refs[:-1], refs[-1]
    rows = table_ref.shape[0]
    strips = scratch.shape[0]
    for channel in range(block):
        spec = nt(table_ref[...], wave_ref[channel])
        for strip in range(strips):
            scratch[strip, pl.ds(channel, rows, stride=block), :] = spec[
                :, strip * LANES : (strip + 1) * LANES
            ]
    pieces = len(outs) // jobs
    per_piece = owners // pieces
    for number, out in enumerate(outs):
        job, piece = number // pieces, number % pieces

        def place(position, carry):
            owner = order_ref[job, piece * per_piece + position]
            start = pl.multiple_of((job * owners + owner) * 2 * block, 2 * block)
            for strip in range(strips):
                span = scratch[strip, pl.ds(start, 2 * block), :]
                out[pl.ds(2 * position, 2), :, strip * LANES : (strip + 1) * LANES] = (
                    span.reshape(2, block, LANES).astype(out.dtype)
                )
            return carry

        lax.fori_loop(0, per_piece, place, 0, unroll=2)


def spectra(orders, table, wave, owners, pieces):
    rows, length = table.shape
    channels, segments, _ = wave.shape
    jobs = rows // (2 * owners)
    block = min(16, channels)
    each = 2 * owners // pieces
    out = jax.ShapeDtypeStruct((each, channels, segments), jnp.bfloat16)
    return pl.pallas_call(
        functools.partial(spectra_kernel, block, owners, jobs),
        grid=(channels // block,),
        in_specs=[
            pl.BlockSpec(memory_space=pltpu.SMEM),
            pl.BlockSpec((rows, length), lambda i: (0, 0)),
            pl.BlockSpec((block, segments, length), lambda i: (i, 0, 0)),
        ],
        out_specs=[pl.BlockSpec((each, block, segments), lambda i: (0, i, 0))] * jobs * pieces,
        out_shape=[out] * jobs * pieces,
        scratch_shapes=[pltpu.VMEM((segments // LANES, rows * block, LANES), jnp.float32)],
        compiler_params=pltpu.CompilerParams(vmem_limit_bytes=VMEM),
        cost_estimate=pl.CostEstimate(
            flops=2 * rows * length * channels * segments,
            bytes_accessed=2 * channels * segments * (length + rows),
            transcendentals=0,
        ),
        name="spectra",
    )(orders, table, wave)


def packed_gram(pieces, scale):
    real = jnp.concatenate([piece[0] for piece in pieces], axis=0)
    imag = jnp.concatenate([piece[1] for piece in pieces], axis=0)
    left = jnp.concatenate([real, imag], axis=0)
    turned = jnp.concatenate([imag, -real], axis=0)
    return (tn(left, left) + tn(left, turned)) * scale


def send_kernel(scale, count, members, *refs):
    for job in range(count):
        pieces = refs[job * members : (job + 1) * members]
        out = refs[count * members + job]
        out[0] = packed_gram(pieces, scale).astype(out.dtype)


def keep_kernel(scale, count, members, *refs):
    came, out = refs[count * members : -1], refs[-1]
    for job in range(count):
        total = packed_gram(refs[job * members : (job + 1) * members], scale)
        if came:
            total = total + came[job][0].astype(jnp.float32)
        out[0, job] = total.astype(out.dtype)


def gram_cost(specs, ends):
    members = len(specs[0])
    _, channels, segments = specs[0][0].shape
    return pl.CostEstimate(
        flops=8 * len(specs) * ends * members * channels * segments * segments,
        bytes_accessed=len(specs)
        * ends
        * (4 * members * channels * segments + 4 * segments * segments),
        transcendentals=0,
    )


def send_gram(specs, ends, scale):
    members = len(specs[0])
    _, channels, segments = specs[0][0].shape
    spec = pl.BlockSpec((2, channels, segments), lambda i: (ends + i, 0, 0))
    return pl.pallas_call(
        functools.partial(send_kernel, scale, len(specs), members),
        grid=(ends,),
        in_specs=[spec] * len(specs) * members,
        out_specs=[pl.BlockSpec((1, segments, segments), lambda i: (i, 0, 0))] * len(specs),
        out_shape=[jax.ShapeDtypeStruct((ends, segments, segments), jnp.bfloat16)] * len(specs),
        compiler_params=pltpu.CompilerParams(vmem_limit_bytes=VMEM),
        cost_estimate=gram_cost(specs, ends),
        name="send_gram",
    )(*sum(specs, []))


def keep_gram(specs, came, ends, scale):
    members = len(specs[0])
    _, channels, segments = specs[0][0].shape
    spec = pl.BlockSpec((2, channels, segments), lambda i: (i, 0, 0))
    each = pl.BlockSpec((1, segments, segments), lambda i: (i, 0, 0))
    jobs = len(specs)
    return pl.pallas_call(
        functools.partial(keep_kernel, scale, jobs, members),
        grid=(ends,),
        in_specs=[spec] * jobs * members + [each] * len(came),
        out_specs=pl.BlockSpec((1, jobs, segments, segments), lambda i: (i, 0, 0, 0)),
        out_shape=jax.ShapeDtypeStruct((ends, jobs, segments, segments), jnp.bfloat16),
        compiler_params=pltpu.CompilerParams(vmem_limit_bytes=VMEM),
        cost_estimate=gram_cost(specs, ends),
        name="keep_gram",
    )(*sum(specs, []), *came)


def split(value):
    high = value.astype(jnp.bfloat16)
    return high, (value - high.astype(jnp.float32)).astype(jnp.bfloat16)


def times_gram(real, imag, high, low):
    rows = real.shape[0]
    vec_high, vec_low = split(jnp.concatenate([real, imag], axis=0))
    straight = nn(vec_high, high) + nn(vec_low, high) + nn(vec_high, low)
    turned = nt(vec_high, high) + nt(vec_low, high) + nt(vec_high, low)
    first, second = straight[:rows], straight[rows:]
    third, fourth = turned[:rows], turned[rows:]
    out_re = 0.5 * (first - second + third + fourth)
    out_im = 0.5 * (first + second + fourth - third)
    return out_re, out_im


def predict_kernel(first, coefs_ref, came_ref, tar_ref, out_ref):
    ends, jobs = came_ref.shape[:2]
    for job in range(jobs):
        packed = came_ref[0, job].astype(jnp.float32)
        for end in range(1, ends):
            packed = packed + came_ref[end, job].astype(jnp.float32)
        high, low = split(packed)
        alpha = coefs_ref[0, first + job]
        beta = coefs_ref[1, first + job]
        tar_re = tar_ref[2 * job].astype(jnp.float32)
        tar_im = tar_ref[2 * job + 1].astype(jnp.float32)
        once_re, once_im = times_gram(tar_re, tar_im, high, low)
        pred_re, pred_im = times_gram(
            alpha * tar_re - beta * once_re, alpha * tar_im - beta * once_im, high, low
        )
        out_ref[2 * job] = pred_re.astype(out_ref.dtype)
        out_ref[2 * job + 1] = pred_im.astype(out_ref.dtype)


def predict(coefs, came, tar, first):
    ends, jobs, segments, _ = came.shape
    targets = tar.shape[1]
    return pl.pallas_call(
        functools.partial(predict_kernel, first),
        grid=(1,),
        in_specs=[
            pl.BlockSpec(memory_space=pltpu.SMEM),
            pl.BlockSpec((ends, jobs, segments, segments), lambda i: (0, 0, 0, 0)),
            pl.BlockSpec((2 * jobs, targets, segments), lambda i: (first // jobs, 0, 0)),
        ],
        out_specs=pl.BlockSpec((2 * jobs, targets, segments), lambda i: (0, 0, 0)),
        out_shape=jax.ShapeDtypeStruct((2 * jobs, targets, segments), jnp.bfloat16),
        compiler_params=pltpu.CompilerParams(vmem_limit_bytes=VMEM),
        cost_estimate=pl.CostEstimate(
            flops=48 * jobs * targets * segments * segments,
            bytes_accessed=2 * ends * jobs * segments * segments,
            transcendentals=0,
        ),
        name="predict",
    )(coefs, came, tar)


def bit_list(number):
    return [1 << place for place in range(number.bit_length() - 1)]


def subsets(bits):
    out = [0]
    for bit in reversed(bits):
        out = [mask | turn for mask in out for turn in (0, bit)]
    return out


def groups_of(devices, bits):
    masks = subsets(sorted(bits))
    every = sum(bits)
    return [[base | mask for mask in masks] for base in range(devices) if not base & every]


def job_orders(outer, inner, channels, segments, per_device):
    low = bit_list(inner)
    high = [bit * inner for bit in bit_list(outer)]
    traded, held = 0, channels
    while traded < len(low) + len(high) and 2 * held <= segments:
        traded, held = traded + 1, 2 * held
    heads = [high[:1] + low + high[1:], high[:1] + low[::-1] + high[1:]]
    jobs = []
    for number in range(per_device):
        order = heads[number % 2]
        jobs.append((order[:traded], order[traded : traded + 1], order[traded + 1 :]))
    return jobs


def local(devices, outer, inner, jobs, width, proof, target, loading):
    channels, segments, length = proof.shape
    targets, span = target.shape[0], target.shape[1]
    half = length // 2
    per_device = half // devices
    rounds = per_device // width
    scale = 1.0 / segments
    rho = (1.0 + math.sqrt(channels * devices / segments)) ** 2
    me = lax.axis_index(AXES)

    def owners_of(job):
        traded, mid, last = job
        fixed, turn = [], []
        for member in subsets(traded):
            for relative in subsets(mid):
                for end in subsets(sorted(last)):
                    fixed.append(end)
                    turn.append(member | relative)
        loose = sum(traded) + sum(mid)
        return (
            jnp.asarray(np.array(fixed, np.int32))
            + jnp.bitwise_xor(me & loose, jnp.asarray(np.array(turn, np.int32)))
        )

    orders = jnp.stack([owners_of(job) for job in jobs])

    def table_of(numbers):
        bins = np.concatenate(
            [np.arange(devices, dtype=np.int64) * per_device + number for number in numbers]
        )
        return forward_rows(bins, length)

    def swap(value, mask):
        return lax.ppermute(value, AXES, [(place, place ^ mask) for place in range(devices)])

    pieces = 2 ** len(jobs[0][0])
    specs = []
    for numbers in (range(width), range(width, per_device)):
        if len(numbers):
            specs += spectra(
                orders[numbers[0] : numbers[-1] + 1],
                table_of(numbers),
                proof,
                devices,
                pieces,
            )

    traded = []
    for number in range(per_device):
        got = []
        for member, mask in enumerate(subsets(jobs[number][0])):
            value = specs[number * pieces + member]
            got.append(swap(value, mask) if mask else value)
        traded.append(got)

    tar_spec = lax.dot_general(
        forward_rows(np.arange(half, dtype=np.int64), length),
        target,
        (((1,), (2,)), ((), ())),
        preferred_element_type=jnp.float32,
    ).astype(jnp.bfloat16)
    tar = lax.all_to_all(tar_spec, AXES, split_axis=0, concat_axis=0, tiled=True)
    tar = tar.reshape(outer, inner, 2 * per_device, targets, span)
    tar = tar.transpose(2, 0, 3, 1, 4).reshape(
        2 * per_device, outer * targets, inner * span
    )
    mine = lax.dynamic_slice_in_dim(loading, me * per_device, per_device)
    step = 1.0 / (mine + rho)
    coefs = jnp.stack([step * (2.0 - step * mine), step * step])

    preds = []
    for number in range(rounds):
        members = range(number * width, (number + 1) * width)
        got = [traded[job] for job in members]
        _, mid, last = jobs[members[0]]
        ends = 2 ** len(last)
        came = []
        if mid:
            sends = send_gram(got, ends, scale)
            for job, send in zip(members, sends):
                bit = jobs[job][1][0]
                came.append(swap(send, bit))
        kept = keep_gram(got, came, ends, scale)
        if last:
            kept = lax.all_to_all(
                kept,
                AXES,
                split_axis=0,
                concat_axis=0,
                tiled=True,
                axis_index_groups=groups_of(devices, last),
            )
        preds.append(predict(coefs, kept, tar, number * width))

    pred = jnp.concatenate(preds, axis=0)
    pred = pred.reshape(2 * per_device, outer, targets, inner, span).transpose(1, 3, 0, 2, 4)
    pred = pred.reshape(devices * 2 * per_device, targets, span)
    returned = lax.all_to_all(pred, AXES, split_axis=0, concat_axis=0, tiled=True)
    return lax.dot_general(
        returned,
        inverse_table(length),
        (((0,), (0,)), ((), ())),
        preferred_element_type=jnp.float32,
    )


def solution(mesh):
    outer, inner = mesh.shape["gx"], mesh.shape["gy"]
    devices = outer * inner

    def whole(proof, target, loading):
        per_device = proof.shape[2] // 2 // devices
        width = 2 if per_device % 2 == 0 else 1
        jobs = job_orders(outer, inner, proof.shape[0] // devices, proof.shape[1], per_device)

        def body(*args):
            return local(devices, outer, inner, jobs, width, *args)

        step = jax.shard_map(
            body,
            mesh=mesh,
            in_specs=(P(AXES, None, None), P("gx", "gy", None), P()),
            out_specs=P("gx", "gy", None),
            check_vma=False,
        )
        return step(proof, target, loading)

    return whole
```
